32 devices in a mesh: chain: 8 (over z, core), bond: 4 (over y, x).
Axes of the slice: x: 2, y: 2, z: 4, core: 2. Of those that a mesh axis runs over, the one named last changes fastest.
Arguments:
- sites: bfloat16 [8, 1024, 2048], P('chain', 'bond'), may hold values from -0.1875 to 0.1875
- start: bfloat16 [8, 1024, 1024], P('chain', 'bond'), may hold values from -0.125 to 0.125
- gates: float32 [8, 16], replicated, may hold values from -3 to 3
- bonds: int32 [9], replicated, may hold values from 512 to 1024, as said below
Outputs:
- new_sites: float32 [8, 1024, 2048], P('chain', 'bond')
The draws below stay inside these ranges and needn't reach their ends.
Inputs may be any that keep to these rules, and one draw needn't show every extreme that they name: bonds[k] is the bond dimension of the cut just left of site k.
All inputs are finite; a program needn't handle non-finite values.
Results may differ from the reference program's by a relative error of at most 0.03.
Values may be sent and summed in bfloat16 or wider, within the bound.
A program may use at most 128 MiB of HBM per device.

```python
import jax
import jax.numpy as jnp
from jax import lax

CHI = 1024
SITES = 8
N_BOND = 4


def draw_bonds(key, part):
    values = jax.random.randint(key, (SITES + 1,), CHI // 2, CHI + 1).astype(jnp.int32)
    values = values.at[0].set(CHI // 2)
    return values.at[SITES // 2].set(CHI)


def levels(key, shape, shards, smallest, top_value):
    factor_of, own = 1.0, jax.random.fold_in(key, 6)
    for position, parts in shards:
        heights = jnp.exp(jax.random.uniform(jax.random.fold_in(own, position), (parts,), jnp.float32, smallest / len(shards), top_value / len(shards)))
        factor_of = factor_of * jnp.repeat(heights, shape[position] // parts).reshape([-1 if axis == position else 1 for axis in range(len(shape))])
    return factor_of


def noise(key, dims, width, limit, cuts=(), held_as=jnp.bfloat16):
    drawn = jax.random.normal(key, dims, jnp.float32) * width
    if len(cuts) > 0:
        drawn = levels(key, dims, cuts, -0.22, 0.18) * drawn
    return jnp.clip(drawn, min=-limit, max=limit).astype(held_as)


def setup_inputs(seed: int = 0) -> dict:
    key_of = jax.random.split(jax.random.key(seed), 5)
    return {
        "sites": noise(key_of[0], (SITES, CHI, 2 * CHI), CHI ** -0.5, 0.1875, ((0, 8), (1, 4))),
        "start": noise(key_of[1], (SITES, CHI, CHI), (2 * CHI) ** -0.5, 0.125, ((0, 8), (1, 4))),
        "gates": noise(key_of[2], (SITES, 16), 0.5, 3.0, (), jnp.float32),
        "bonds": draw_bonds(jax.random.fold_in(key_of[4], 71), 0),
    }


ridge_ratio = 0.05

def pair_update(left_tensor, right_tensor, start_low, start_high, gate_row, bond_left, bond_mid, bond_right):
    columns = jnp.arange(CHI)
    mid_keep = columns < bond_mid
    right_keep = columns < bond_right
    left_keep = (columns < bond_left)[:, None] & jnp.tile(mid_keep, 2)[None, :]
    left_used = jnp.where(left_keep, left_tensor, jnp.zeros((), jnp.bfloat16))
    right_used = jnp.where(jnp.tile(right_keep, 2)[None, :], right_tensor, jnp.zeros((), jnp.bfloat16))
    mix_zero = jnp.dot(left_used[:, :CHI].astype(jnp.float32), right_used.astype(jnp.float32), preferred_element_type=jnp.float32)
    mix_one = jnp.dot(left_used[:, CHI:].astype(jnp.float32), right_used.astype(jnp.float32), preferred_element_type=jnp.float32)
    gate_matrix = gate_row.reshape(4, 4)
    theta_list = []
    for out_row in range(2):
        pieces = []
        for out_col in range(2):
            coeffs = gate_matrix[2 * out_row + out_col]
            pieces.append(coeffs[0] * mix_zero[:, :CHI] + coeffs[1] * mix_zero[:, CHI:] + coeffs[2] * mix_one[:, :CHI] + coeffs[3] * mix_one[:, CHI:])
        theta_list.append(jnp.concatenate(pieces, axis=1).astype(jnp.bfloat16))
    basis_start = jnp.where(mid_keep[None, :], jnp.concatenate([start_low, start_high], axis=0), jnp.zeros((), jnp.bfloat16))
    local_rows = CHI // N_BOND
    summed = jnp.zeros((2 * CHI, CHI), jnp.float32)
    for theta_rows in theta_list:
        image_rows = jnp.dot(theta_rows.astype(jnp.float32), basis_start.astype(jnp.float32), preferred_element_type=jnp.float32).astype(jnp.bfloat16)
        split_theta = theta_rows.reshape(N_BOND, local_rows, 2 * CHI).astype(jnp.float32)
        split_image = image_rows.reshape(N_BOND, local_rows, CHI).astype(jnp.float32)
        block_terms = jnp.einsum('kar,kas->krs', split_theta, split_image)
        rounded = lax.optimization_barrier(block_terms.astype(jnp.bfloat16))
        summed = summed + lax.optimization_barrier(jnp.sum(rounded.astype(jnp.float32), axis=0))
    projected = summed
    gram_matrix = lax.dot_general(projected.astype(jnp.float32), projected.astype(jnp.float32), (((0,), (0,)), ((), ())), precision=lax.Precision.HIGHEST, preferred_element_type=jnp.float32)
    trace_sum = jnp.sum(jnp.diagonal(gram_matrix))
    kept_count = jnp.sum(mid_keep.astype(jnp.float32))
    added = jnp.where(mid_keep, ridge_ratio * trace_sum / kept_count, 1.0).astype(jnp.float32)
    factor = jnp.linalg.cholesky(gram_matrix + jnp.diag(added))
    exact_basis = lax.linalg.triangular_solve(factor, projected, left_side=False, lower=True, transpose_a=True)
    basis_new = exact_basis.astype(jnp.bfloat16)
    upper_rows = jnp.concatenate([jnp.dot(theta_rows.astype(jnp.float32), basis_new.astype(jnp.float32), preferred_element_type=jnp.float32) for theta_rows in theta_list], axis=1)
    sum_squares = jnp.sum(upper_rows * upper_rows)
    mean_square = sum_squares / (2.0 * bond_left.astype(jnp.float32) * bond_mid.astype(jnp.float32)) + 1e-06
    new_left = upper_rows * lax.rsqrt(mean_square)
    new_right = jnp.sqrt(2.0 * bond_right.astype(jnp.float32)) * exact_basis.T
    return (new_left, new_right)

def reference(sites, start, gates, bonds):
    updated = jnp.zeros((SITES, CHI, 2 * CHI), jnp.float32)

    def apply_pair(current, pair_index):
        left_site = (2 * pair_index).astype(jnp.int32)
        new_left, new_right = pair_update(sites[left_site], sites[left_site + 1], start[left_site], start[left_site + 1], gates[left_site], bonds[left_site], bonds[left_site + 1], bonds[left_site + 2])
        current = lax.dynamic_update_index_in_dim(current, new_left, left_site, 0)
        current = lax.dynamic_update_index_in_dim(current, new_right, (left_site + 1).astype(jnp.int32), 0)
        return (current, None)
    updated, _ = lax.scan(apply_pair, updated, jnp.arange(SITES // 2).astype(jnp.int32))
    return updated
```

```python
import jax
import jax.numpy as jnp
from jax import lax
from jax.experimental import pallas as pl
from jax.experimental.pallas import tpu as pltpu
from jax.sharding import PartitionSpec as P

ridge_ratio = 0.05
BLOCK = 128
SUB = 8


def partner(value, axis, apart):
    return lax.ppermute(value, axis, [(i, i ^ 1 << apart) for i in range(lax.axis_size(axis))])


def halves(x):
    high = x.astype(jnp.bfloat16)
    return high, (x - high.astype(jnp.float32)).astype(jnp.bfloat16)


def diagonal_inverse(tile):
    lane = lax.broadcasted_iota(jnp.int32, (SUB, BLOCK), 1)
    sub = lax.broadcasted_iota(jnp.int32, (SUB, BLOCK), 0)
    count = BLOCK // SUB
    rows = [tile[i * SUB : (i + 1) * SUB, :] for i in range(count)]
    full = (SUB, BLOCK)
    for b in range(count):
        base = b * SUB
        cols = [jnp.broadcast_to(rows[b][:, base + j : base + j + 1], full) for j in range(SUB)]
        current = rows[b]
        scale = jnp.zeros(full, jnp.float32)
        inverses, uppers, finals = [], {}, []
        for j in range(SUB):
            pivot = jnp.broadcast_to(cols[j][j : j + 1, :], full)
            inv = 1.0 / pivot
            inverses.append(inv)
            scale = jnp.where(sub == j, pivot, scale)
            m = jnp.where(sub > j, cols[j] * inv, 0.0)
            for k in range(j + 1, SUB):
                uppers[j, k] = jnp.broadcast_to(cols[k][j : j + 1, :], full)
                cols[k] = cols[k] - m * uppers[j, k]
            row = jnp.broadcast_to(current[j : j + 1, :], full)
            row = jnp.where(lane == base + j, 1.0, row)
            finals.append(jnp.where((lane > base + j) & (lane < base + SUB), 0.0, row))
            current = jnp.where((lane == base + j) & (sub >= j), jnp.where(sub == j, 1.0, 0.0), current) - m * row
        inside = (lane >= base) & (lane < base + SUB)
        for i in range(b + 1, count):
            held = [jnp.broadcast_to(rows[i][:, base + j : base + j + 1], full) for j in range(SUB)]
            fresh = jnp.where(inside, 0.0, rows[i])
            for j in range(SUB):
                c = held[j] * inverses[j]
                for k in range(j + 1, SUB):
                    held[k] = held[k] - c * uppers[j, k]
                fresh = fresh - c * finals[j]
            rows[i] = fresh
        rows[b] = jnp.where(lane <= base + sub, current * lax.rsqrt(scale), 0.0)
    return jnp.concatenate(rows, axis=0)


def factor_kernel(gram_ref, out_ref, right_ref):
    size = gram_ref.shape[0]
    count = size // BLOCK

    def copy(i, carry):
        here = pl.ds(pl.multiple_of(i * BLOCK, BLOCK), BLOCK)
        out_ref[here, :] = gram_ref[here, :]
        return carry

    lax.fori_loop(0, count, copy, 0)

    def panel(k, carry):
        here = pl.ds(pl.multiple_of(k * BLOCK, BLOCK), BLOCK)
        inverse = diagonal_inverse(out_ref[here, here])
        inv_high, inv_low = halves(inverse)
        row_high, row_low = halves(out_ref[here, :])
        out_ref[here, :] = jnp.dot(
            jnp.concatenate([inv_high, inv_high, inv_low], axis=1),
            jnp.concatenate([row_high, row_low, row_high], axis=0),
            preferred_element_type=jnp.float32,
        )
        out_ref[here, here] = inverse
        high, low = halves(out_ref[here, :])
        right_ref[0:BLOCK, :] = high
        right_ref[BLOCK : 2 * BLOCK, :] = low
        right_ref[2 * BLOCK : 3 * BLOCK, :] = high

        def trailing(i, inner):
            there = pl.ds(pl.multiple_of(i * BLOCK, BLOCK), BLOCK)
            left_high, left_low = halves(out_ref[here, there].T)
            out_ref[there, here] = jnp.zeros((BLOCK, BLOCK), jnp.float32)
            out_ref[there, :] = out_ref[there, :] - jnp.dot(
                jnp.concatenate([left_high, left_high, left_low], axis=1),
                right_ref[...],
                preferred_element_type=jnp.float32,
            )
            return inner

        lax.fori_loop(k + 1, count, trailing, 0)
        column = lax.broadcasted_iota(jnp.int32, (BLOCK, size), 1)
        out_ref[here, :] = jnp.where(column < (k + 1) * BLOCK, out_ref[here, :], 0.0)
        return carry

    lax.fori_loop(0, count, panel, 0)


def factor_inverse(shifted):
    size = shifted.shape[0]
    return pl.pallas_call(
        factor_kernel,
        out_shape=jax.ShapeDtypeStruct((size, size), jnp.float32),
        in_specs=[pl.BlockSpec(memory_space=pltpu.VMEM)],
        out_specs=pl.BlockSpec(memory_space=pltpu.VMEM),
        scratch_shapes=[pltpu.VMEM((3 * BLOCK, size), jnp.bfloat16)],
    )(shifted)


def local(sites, start, gates, bonds):
    bond_index = lax.axis_index("bond")
    chain_index = lax.axis_index("chain")
    rank_width = start.shape[2]
    local_rows = sites.shape[1]
    own_site = sites[0]
    own_start = start[0]
    is_left = chain_index % 2 == 0
    left_site = jnp.where(is_left, chain_index, chain_index - 1)
    bond_left = bonds[left_site]
    bond_mid = bonds[left_site + 1]
    bond_right = bonds[left_site + 2]
    columns = jnp.arange(rank_width)
    row_global = bond_index * local_rows + jnp.arange(local_rows)
    mid_keep = columns < bond_mid
    right_keep = columns < bond_right
    whole_site, whole_start = (
        lax.all_gather(own_site, "bond", axis=0, tiled=True),
        lax.all_gather(own_start, "bond", axis=0, tiled=True),
    )
    other_site, other_start = partner((whole_site, whole_start), "chain", 0)
    b_full, start_zero, start_one = lax.cond(
        is_left,
        lambda: (other_site, whole_start, other_start),
        lambda: (whole_site, other_start, whole_start),
    )
    other_rows = lax.dynamic_slice_in_dim(other_site, bond_index * local_rows, local_rows, 0)
    a_rows = jnp.where(is_left, own_site, other_rows)
    left_keep = (row_global < bond_left)[:, None] & jnp.tile(mid_keep, 2)[None, :]
    left_used = jnp.where(left_keep, a_rows, jnp.zeros((), jnp.bfloat16))
    pair_keep = jnp.tile(right_keep, 2)[None, :]
    mix_zero = jnp.where(
        pair_keep,
        jnp.dot(left_used[:, :rank_width], b_full, preferred_element_type=jnp.float32),
        0.0,
    )
    mix_one = jnp.where(
        pair_keep,
        jnp.dot(left_used[:, rank_width:], b_full, preferred_element_type=jnp.float32),
        0.0,
    )
    gate_matrix = gates[left_site].reshape(4, 4)

    def theta_for(out_row):
        gate_rows = lax.dynamic_slice_in_dim(gate_matrix, 2 * out_row, 2, 0)
        pieces = []
        for out_col in range(2):
            coeffs = gate_rows[out_col]
            pieces.append(
                coeffs[0] * mix_zero[:, :rank_width]
                + coeffs[1] * mix_zero[:, rank_width:]
                + coeffs[2] * mix_one[:, :rank_width]
                + coeffs[3] * mix_one[:, rank_width:]
            )
        return jnp.concatenate(pieces, axis=1).astype(jnp.bfloat16)

    theta_rows = theta_for(jnp.where(is_left, 0, 1))
    theta_second = theta_for(1)
    image_full = jnp.dot(
        theta_rows[:, :rank_width], start_zero, preferred_element_type=jnp.float32
    ) + jnp.dot(theta_rows[:, rank_width:], start_one, preferred_element_type=jnp.float32)
    image_rows = jnp.where(mid_keep[None, :], image_full, 0.0).astype(jnp.bfloat16)
    own = lax.dot_general(
        theta_rows, image_rows, (((0,), (0,)), ((), ())), preferred_element_type=jnp.float32
    ).astype(jnp.bfloat16)
    kept_half = jnp.where(is_left, 0, 1)
    half_rows = own.shape[0] // 2
    kept = lax.dynamic_slice_in_dim(own, kept_half * half_rows, half_rows, 0)
    given = lax.dynamic_slice_in_dim(own, (1 - kept_half) * half_rows, half_rows, 0)
    both = (kept.astype(jnp.float32) + partner(given, "chain", 0).astype(jnp.float32)).astype(jnp.bfloat16)
    summed = lax.psum_scatter(both, "bond", scatter_dimension=0, tiled=True)
    own_half = lax.all_gather(summed, "bond", axis=0, tiled=True)
    other_half = partner(own_half, "chain", 0)
    projected_all = jnp.concatenate(
        [jnp.where(is_left, own_half, other_half), jnp.where(is_left, other_half, own_half)], axis=0
    )
    gram = lax.dot_general(
        projected_all, projected_all, (((0,), (0,)), ((), ())), preferred_element_type=jnp.float32
    )
    eye = jnp.arange(rank_width)[:, None] == jnp.arange(rank_width)[None, :]
    trace_sum = jnp.sum(jnp.where(eye, gram, 0.0))
    added = jnp.where(mid_keep, ridge_ratio * trace_sum / bond_mid.astype(jnp.float32), 1.0)
    inverse = factor_inverse(gram + jnp.where(eye, added[None, :], 0.0))

    def left_rows():
        pieces = []
        for theta in (theta_rows, theta_second):
            reduced = jnp.dot(theta, projected_all, preferred_element_type=jnp.float32)
            pieces.append(
                lax.dot_general(
                    reduced,
                    inverse,
                    (((1,), (1,)), ((), ())),
                    precision=lax.Precision.HIGH,
                    preferred_element_type=jnp.float32,
                )
            )
        joined = jnp.concatenate(pieces, axis=1)
        return joined, jnp.sum(joined * joined)

    def right_rows():
        block = lax.dynamic_slice_in_dim(inverse, bond_index * local_rows, local_rows, 0)
        basis_rows = lax.dot_general(
            block,
            projected_all.astype(jnp.float32),
            (((1,), (1,)), ((), ())),
            precision=lax.Precision.HIGH,
            preferred_element_type=jnp.float32,
        )
        return basis_rows, jnp.float32(0.0)

    rows, squares = lax.cond(is_left, left_rows, right_rows)
    sum_squares = lax.psum(squares, "bond")
    mean_square = (
        sum_squares / (2.0 * bond_left.astype(jnp.float32) * bond_mid.astype(jnp.float32)) + 1e-06
    )
    factor = jnp.where(
        is_left, lax.rsqrt(mean_square), jnp.sqrt(2.0 * bond_right.astype(jnp.float32))
    )
    return (rows * factor)[None]


def solution(mesh):
    placed = (P("chain", "bond", None), P("chain", "bond", None), P(), P())
    return jax.shard_map(
        local, mesh=mesh, in_specs=placed, out_specs=P("chain", "bond", None), check_vma=False
    )
```

```python
import jax
import jax.numpy as jnp
from jax import lax
from jax.experimental import pallas as pl
from jax.experimental.pallas import tpu as pltpu
from jax.sharding import PartitionSpec as P

ridge_ratio = 0.05
BLOCK = 128
SUB = 8


def partner(value, axis, apart):
    return lax.ppermute(value, axis, [(i, i ^ 1 << apart) for i in range(lax.axis_size(axis))])


def halves(x):
    high = x.astype(jnp.bfloat16)
    return high, (x - high.astype(jnp.float32)).astype(jnp.bfloat16)


def diagonal_inverse(tile):
    lane = lax.broadcasted_iota(jnp.int32, (SUB, BLOCK), 1)
    sub = lax.broadcasted_iota(jnp.int32, (SUB, BLOCK), 0)
    count = BLOCK // SUB
    rows = [tile[i * SUB : (i + 1) * SUB, :] for i in range(count)]
    full = (SUB, BLOCK)
    for b in range(count):
        base = b * SUB
        cols = [jnp.broadcast_to(rows[b][:, base + j : base + j + 1], full) for j in range(SUB)]
        current = rows[b]
        scale = jnp.zeros(full, jnp.float32)
        inverses, uppers, finals = [], {}, []
        for j in range(SUB):
            pivot = jnp.broadcast_to(cols[j][j : j + 1, :], full)
            inv = 1.0 / pivot
            inverses.append(inv)
            scale = jnp.where(sub == j, pivot, scale)
            m = jnp.where(sub > j, cols[j] * inv, 0.0)
            for k in range(j + 1, SUB):
                uppers[j, k] = jnp.broadcast_to(cols[k][j : j + 1, :], full)
                cols[k] = cols[k] - m * uppers[j, k]
            row = jnp.broadcast_to(current[j : j + 1, :], full)
            row = jnp.where(lane == base + j, 1.0, row)
            finals.append(jnp.where((lane > base + j) & (lane < base + SUB), 0.0, row))
            current = jnp.where((lane == base + j) & (sub >= j), jnp.where(sub == j, 1.0, 0.0), current) - m * row
        inside = (lane >= base) & (lane < base + SUB)
        for i in range(b + 1, count):
            held = [jnp.broadcast_to(rows[i][:, base + j : base + j + 1], full) for j in range(SUB)]
            fresh = jnp.where(inside, 0.0, rows[i])
            for j in range(SUB):
                c = held[j] * inverses[j]
                for k in range(j + 1, SUB):
                    held[k] = held[k] - c * uppers[j, k]
                fresh = fresh - c * finals[j]
            rows[i] = fresh
        rows[b] = jnp.where(lane <= base + sub, current * lax.rsqrt(scale), 0.0)
    return jnp.concatenate(rows, axis=0)


def factor_kernel(gram_ref, out_ref, right_ref):
    size = gram_ref.shape[0]
    count = size // BLOCK

    def copy(i, carry):
        here = pl.ds(pl.multiple_of(i * BLOCK, BLOCK), BLOCK)
        out_ref[here, :] = gram_ref[here, :]
        return carry

    lax.fori_loop(0, count, copy, 0)

    def panel(k, carry):
        here = pl.ds(pl.multiple_of(k * BLOCK, BLOCK), BLOCK)
        inverse = diagonal_inverse(out_ref[here, here])
        inv_high, inv_low = halves(inverse)
        row_high, row_low = halves(out_ref[here, :])
        out_ref[here, :] = jnp.dot(
            jnp.concatenate([inv_high, inv_high, inv_low], axis=1),
            jnp.concatenate([row_high, row_low, row_high], axis=0),
            preferred_element_type=jnp.float32,
        )
        out_ref[here, here] = inverse
        high, low = halves(out_ref[here, :])
        right_ref[0:BLOCK, :] = high
        right_ref[BLOCK : 2 * BLOCK, :] = low
        right_ref[2 * BLOCK : 3 * BLOCK, :] = high

        def trailing(i, inner):
            there = pl.ds(pl.multiple_of(i * BLOCK, BLOCK), BLOCK)
            left_high, left_low = halves(out_ref[here, there].T)
            out_ref[there, here] = jnp.zeros((BLOCK, BLOCK), jnp.float32)
            out_ref[there, :] = out_ref[there, :] - jnp.dot(
                jnp.concatenate([left_high, left_high, left_low], axis=1),
                right_ref[...],
                preferred_element_type=jnp.float32,
            )
            return inner

        lax.fori_loop(k + 1, count, trailing, 0)
        column = lax.broadcasted_iota(jnp.int32, (BLOCK, size), 1)
        out_ref[here, :] = jnp.where(column < (k + 1) * BLOCK, out_ref[here, :], 0.0)
        return carry

    lax.fori_loop(0, count, panel, 0)


def factor_inverse(shifted):
    size = shifted.shape[0]
    return pl.pallas_call(
        factor_kernel,
        out_shape=jax.ShapeDtypeStruct((size, size), jnp.float32),
        in_specs=[pl.BlockSpec(memory_space=pltpu.VMEM)],
        out_specs=pl.BlockSpec(memory_space=pltpu.VMEM),
        scratch_shapes=[pltpu.VMEM((3 * BLOCK, size), jnp.bfloat16)],
    )(shifted)


MESH = pl.DeviceIdType.MESH


class Links:
    def __init__(self, send_sem, recv_sem):
        self.chain, self.me = lax.axis_index("chain"), lax.axis_index("bond")
        self.core = self.chain % 2
        self.near = self.me + 1 - 2 * (self.me % 2)
        self.far = (self.me + 2) % 4
        self.across = 3 - self.me
        self.x, self.y, self.d = (self.chain, self.near), (self.chain, self.far), (self.chain, self.across)
        self.mate = (self.chain + 1 - 2 * self.core, self.me)
        self.send_sem, self.recv_sem, self.copies = send_sem, recv_sem, []

    def greet(self, others):
        barrier = pltpu.get_barrier_semaphore()
        for other in others:
            pl.semaphore_signal(barrier, inc=1, device_id=other, device_id_type=MESH)
        pl.semaphore_wait(barrier, len(others))

    def send(self, source, target, device):
        slot = len(self.copies)
        copy = pltpu.make_async_remote_copy(
            src_ref=source,
            dst_ref=target,
            send_sem=self.send_sem.at[slot],
            recv_sem=self.recv_sem.at[slot],
            device_id=device,
            device_id_type=MESH,
        )
        copy.start()
        self.copies.append(copy)
        return copy

    def spread(self, first_own, second_own, first, second):
        s0 = self.send(second_own, second(self.me), self.x)
        f0 = self.send(first_own, first(self.me), self.y)
        f1 = self.send(first_own, first(self.me), self.x)
        s1 = self.send(second_own, second(self.me), self.y)
        f0.wait_recv()
        f2 = self.send(first(self.far), first(self.far), self.x)
        late = [self.send(first(self.far), first(self.far), self.mate)]
        s0.wait_recv()
        s2 = self.send(second(self.near), second(self.near), self.y)
        late.append(self.send(second(self.near), second(self.near), self.mate))
        f1.wait_recv()
        late.append(self.send(first(self.near), first(self.near), self.mate))
        s1.wait_recv()
        late.append(self.send(second(self.far), second(self.far), self.mate))
        f2.wait_recv()
        late.append(self.send(first(self.across), first(self.across), self.mate))
        s2.wait_recv()
        late.append(self.send(second(self.across), second(self.across), self.mate))
        for copy in late:
            copy.wait_recv()

    def drain(self):
        for copy in self.copies:
            copy.wait_send()


def gather_kernel(b_ref, s_ref, b_out, s_out, send_sem, recv_sem, local_sem):
    links = Links(send_sem, recv_sem)
    links.greet((links.x, links.y, links.mate))
    core, me = links.core, links.me
    kept_b = pltpu.make_async_copy(b_ref, b_out.at[me], local_sem.at[0])
    kept_s = pltpu.make_async_copy(s_ref, s_out.at[core, me], local_sem.at[1])
    own = links.send(s_ref, s_out.at[core, me], links.mate)
    kept_b.start()
    kept_s.start()
    links.spread(
        b_ref.at[core], s_ref, lambda i: b_out.at[i, core], lambda i: s_out.at[core, i]
    )
    own.wait_recv()
    links.drain()
    kept_b.wait()
    kept_s.wait()


def gather_pair(b_rows, own_start):
    rows, wide = b_rows.shape
    width = own_start.shape[1]
    n = lax.axis_size("bond")
    b_full, starts = pl.pallas_call(
        gather_kernel,
        out_shape=(
            jax.ShapeDtypeStruct((n, 2, rows // 2, wide), b_rows.dtype),
            jax.ShapeDtypeStruct((2, n, rows, width), own_start.dtype),
        ),
        in_specs=[pl.BlockSpec(memory_space=pltpu.VMEM)] * 2,
        out_specs=(pl.BlockSpec(memory_space=pl.ANY),) * 2,
        scratch_shapes=[
            pltpu.SemaphoreType.DMA((13,)),
            pltpu.SemaphoreType.DMA((13,)),
            pltpu.SemaphoreType.DMA((2,)),
        ],
        compiler_params=pltpu.CompilerParams(collective_id=0, has_side_effects=True),
    )(b_rows.reshape(2, rows // 2, wide), own_start)
    return b_full.reshape(n * rows, wide), starts.reshape(2, n * rows, width)


def reduce_kernel(own_ref, out_ref, inc, acc, one, two, send_sem, recv_sem):
    links = Links(send_sem, recv_sem)
    links.greet((links.x, links.y, links.mate))
    core, me, near, far, across = links.core, links.me, links.near, links.far, links.across
    half = own_ref.shape[2] // 2
    low, high = pl.ds(0, half), pl.ds(half, half)
    order = (across, near, far, me)
    swaps = [links.send(own_ref.at[1 - core, i], inc.at[i], links.mate) for i in order]

    def merge(position):
        i = order[position]
        swaps[position].wait_recv()
        acc[i] = (own_ref[core, i].astype(jnp.float32) + inc[i].astype(jnp.float32)).astype(jnp.bfloat16)

    merge(0)
    x1 = links.send(acc.at[across, low], one.at[0, 1], links.x)
    y1 = links.send(acc.at[across, high], one.at[1, 1], links.y)
    merge(1)
    x0 = links.send(acc.at[near, low], one.at[0, 0], links.x)
    merge(2)
    y0 = links.send(acc.at[far, high], one.at[1, 0], links.y)
    merge(3)
    x1.wait_recv()
    two[2] = (acc[far, low].astype(jnp.float32) + one[0, 1].astype(jnp.float32)).astype(jnp.bfloat16)
    y2 = links.send(two.at[2], two.at[0], links.y)
    y1.wait_recv()
    two[3] = (acc[near, high].astype(jnp.float32) + one[1, 1].astype(jnp.float32)).astype(jnp.bfloat16)
    x2 = links.send(two.at[3], two.at[1], links.x)
    x0.wait_recv()
    y2.wait_recv()
    out_ref[core, me, low] = (
        acc[me, low].astype(jnp.float32) + one[0, 0].astype(jnp.float32) + two[0].astype(jnp.float32)
    ).astype(jnp.bfloat16)
    y0.wait_recv()
    x2.wait_recv()
    out_ref[core, me, high] = (
        acc[me, high].astype(jnp.float32) + one[1, 0].astype(jnp.float32) + two[1].astype(jnp.float32)
    ).astype(jnp.bfloat16)
    own = links.send(out_ref.at[core, me], out_ref.at[core, me], links.mate)
    links.spread(
        out_ref.at[core, me, low],
        out_ref.at[core, me, high],
        lambda i: out_ref.at[core, i, low],
        lambda i: out_ref.at[core, i, high],
    )
    own.wait_recv()
    links.drain()


def reduce_pair(own):
    total, width = own.shape
    n = lax.axis_size("bond")
    rows = total // (2 * n)
    whole = pl.pallas_call(
        reduce_kernel,
        out_shape=jax.ShapeDtypeStruct((2, n, rows, width), own.dtype),
        in_specs=[pl.BlockSpec(memory_space=pltpu.VMEM)],
        out_specs=pl.BlockSpec(memory_space=pltpu.VMEM),
        scratch_shapes=[
            pltpu.VMEM((n, rows, width), own.dtype),
            pltpu.VMEM((n, rows, width), own.dtype),
            pltpu.VMEM((2, 2, rows // 2, width), own.dtype),
            pltpu.VMEM((4, rows // 2, width), own.dtype),
            pltpu.SemaphoreType.DMA((23,)),
            pltpu.SemaphoreType.DMA((23,)),
        ],
        compiler_params=pltpu.CompilerParams(collective_id=1, has_side_effects=True),
    )(own.reshape(2, n, rows, width))
    return whole.reshape(total, width)


def total_kernel(value_ref, out_ref, held, send_sem, recv_sem):
    links = Links(send_sem, recv_sem)
    others = (links.x, links.y, links.d)
    links.greet(others)
    copies = [links.send(value_ref, held.at[i], other) for i, other in enumerate(others)]
    for copy in copies:
        copy.wait_recv()
    out_ref[...] = (value_ref[...] + held[2]) + (held[0] + held[1])
    links.drain()


def total_of(value):
    shape = (8, 128)
    return pl.pallas_call(
        total_kernel,
        out_shape=jax.ShapeDtypeStruct(shape, jnp.float32),
        in_specs=[pl.BlockSpec(memory_space=pltpu.VMEM)],
        out_specs=pl.BlockSpec(memory_space=pltpu.VMEM),
        scratch_shapes=[
            pltpu.VMEM((3,) + shape, jnp.float32),
            pltpu.SemaphoreType.DMA((3,)),
            pltpu.SemaphoreType.DMA((3,)),
        ],
        compiler_params=pltpu.CompilerParams(collective_id=2, has_side_effects=True),
    )(jnp.full(shape, value, jnp.float32))[0, 0]


def local(sites, start, gates, bonds):
    bond_index = lax.axis_index("bond")
    chain_index = lax.axis_index("chain")
    rank_width = start.shape[2]
    local_rows = sites.shape[1]
    own_site = sites[0]
    own_start = start[0]
    is_left = chain_index % 2 == 0
    left_site = jnp.where(is_left, chain_index, chain_index - 1)
    bond_left = bonds[left_site]
    bond_mid = bonds[left_site + 1]
    bond_right = bonds[left_site + 2]
    columns = jnp.arange(rank_width)
    row_global = bond_index * local_rows + jnp.arange(local_rows)
    mid_keep = columns < bond_mid
    right_keep = columns < bond_right
    other_rows = partner(own_site, "chain", 0)
    a_rows = jnp.where(is_left, own_site, other_rows)
    b_rows = jnp.where(is_left, other_rows, own_site)
    square = lax.axis_size("bond") == 4
    if square:
        b_full, starts = gather_pair(b_rows, own_start)
    else:
        b_full = lax.all_gather(b_rows, "bond", axis=0, tiled=True)
        whole_start = lax.all_gather(own_start, "bond", axis=0, tiled=True)
        other_start = partner(whole_start, "chain", 0)
        starts = jnp.stack(
            [jnp.where(is_left, whole_start, other_start), jnp.where(is_left, other_start, whole_start)]
        )
    start_zero, start_one = starts[0], starts[1]
    left_keep = (row_global < bond_left)[:, None] & jnp.tile(mid_keep, 2)[None, :]
    left_used = jnp.where(left_keep, a_rows, jnp.zeros((), jnp.bfloat16))
    pair_keep = jnp.tile(right_keep, 2)[None, :]
    mix_zero = jnp.where(
        pair_keep,
        jnp.dot(left_used[:, :rank_width], b_full, preferred_element_type=jnp.float32),
        0.0,
    )
    mix_one = jnp.where(
        pair_keep,
        jnp.dot(left_used[:, rank_width:], b_full, preferred_element_type=jnp.float32),
        0.0,
    )
    gate_matrix = gates[left_site].reshape(4, 4)

    def theta_for(out_row):
        gate_rows = lax.dynamic_slice_in_dim(gate_matrix, 2 * out_row, 2, 0)
        pieces = []
        for out_col in range(2):
            coeffs = gate_rows[out_col]
            pieces.append(
                coeffs[0] * mix_zero[:, :rank_width]
                + coeffs[1] * mix_zero[:, rank_width:]
                + coeffs[2] * mix_one[:, :rank_width]
                + coeffs[3] * mix_one[:, rank_width:]
            )
        return jnp.concatenate(pieces, axis=1).astype(jnp.bfloat16)

    theta_rows = theta_for(jnp.where(is_left, 0, 1))
    theta_second = theta_for(1)
    image_full = jnp.dot(
        theta_rows[:, :rank_width], start_zero, preferred_element_type=jnp.float32
    ) + jnp.dot(theta_rows[:, rank_width:], start_one, preferred_element_type=jnp.float32)
    image_rows = jnp.where(mid_keep[None, :], image_full, 0.0).astype(jnp.bfloat16)
    own = lax.dot_general(
        theta_rows, image_rows, (((0,), (0,)), ((), ())), preferred_element_type=jnp.float32
    ).astype(jnp.bfloat16)
    if square:
        projected_all = reduce_pair(own)
    else:
        kept_half = jnp.where(is_left, 0, 1)
        half_rows = own.shape[0] // 2
        kept = lax.dynamic_slice_in_dim(own, kept_half * half_rows, half_rows, 0)
        given = lax.dynamic_slice_in_dim(own, (1 - kept_half) * half_rows, half_rows, 0)
        both = (kept.astype(jnp.float32) + partner(given, "chain", 0).astype(jnp.float32)).astype(jnp.bfloat16)
        summed = lax.psum_scatter(both, "bond", scatter_dimension=0, tiled=True)
        own_half = lax.all_gather(summed, "bond", axis=0, tiled=True)
        other_half = partner(own_half, "chain", 0)
        projected_all = jnp.concatenate(
            [jnp.where(is_left, own_half, other_half), jnp.where(is_left, other_half, own_half)], axis=0
        )
    gram = lax.dot_general(
        projected_all, projected_all, (((0,), (0,)), ((), ())), preferred_element_type=jnp.float32
    )
    eye = jnp.arange(rank_width)[:, None] == jnp.arange(rank_width)[None, :]
    trace_sum = jnp.sum(jnp.where(eye, gram, 0.0))
    added = jnp.where(mid_keep, ridge_ratio * trace_sum / bond_mid.astype(jnp.float32), 1.0)
    inverse = factor_inverse(gram + jnp.where(eye, added[None, :], 0.0))

    def left_rows():
        pieces = []
        for theta in (theta_rows, theta_second):
            reduced = jnp.dot(theta, projected_all, preferred_element_type=jnp.float32)
            pieces.append(
                lax.dot_general(
                    reduced,
                    inverse,
                    (((1,), (1,)), ((), ())),
                    precision=lax.Precision.HIGH,
                    preferred_element_type=jnp.float32,
                )
            )
        joined = jnp.concatenate(pieces, axis=1)
        return joined, jnp.sum(joined * joined)

    def right_rows():
        block = lax.dynamic_slice_in_dim(inverse, bond_index * local_rows, local_rows, 0)
        basis_rows = lax.dot_general(
            block,
            projected_all.astype(jnp.float32),
            (((1,), (1,)), ((), ())),
            precision=lax.Precision.HIGH,
            preferred_element_type=jnp.float32,
        )
        return basis_rows, jnp.float32(0.0)

    rows, squares = lax.cond(is_left, left_rows, right_rows)
    sum_squares = total_of(squares) if square else lax.psum(squares, "bond")
    mean_square = (
        sum_squares / (2.0 * bond_left.astype(jnp.float32) * bond_mid.astype(jnp.float32)) + 1e-06
    )
    factor = jnp.where(
        is_left, lax.rsqrt(mean_square), jnp.sqrt(2.0 * bond_right.astype(jnp.float32))
    )
    return (rows * factor)[None]


def solution(mesh):
    placed = (P("chain", "bond", None), P("chain", "bond", None), P(), P())
    return jax.shard_map(
        local, mesh=mesh, in_specs=placed, out_specs=P("chain", "bond", None), check_vma=False
    )
```

```python
import jax
import jax.numpy as jnp
from jax import lax
from jax.experimental import pallas as pl
from jax.experimental.pallas import tpu as pltpu
from jax.sharding import PartitionSpec as P

ridge_ratio = 0.05
BLOCK = 128
SUB = 8


def partner(value, axis, apart):
    return lax.ppermute(value, axis, [(i, i ^ 1 << apart) for i in range(lax.axis_size(axis))])


def halves(x):
    high = x.astype(jnp.bfloat16)
    return high, (x - high.astype(jnp.float32)).astype(jnp.bfloat16)


def diagonal_inverse(tile):
    lane = lax.broadcasted_iota(jnp.int32, (SUB, BLOCK), 1)
    sub = lax.broadcasted_iota(jnp.int32, (SUB, BLOCK), 0)
    count = BLOCK // SUB
    rows = [tile[i * SUB : (i + 1) * SUB, :] for i in range(count)]
    full = (SUB, BLOCK)
    for b in range(count):
        base = b * SUB
        cols = [jnp.broadcast_to(rows[b][:, base + j : base + j + 1], full) for j in range(SUB)]
        current = rows[b]
        scale = jnp.zeros(full, jnp.float32)
        inverses, uppers, finals = [], {}, []
        for j in range(SUB):
            pivot = jnp.broadcast_to(cols[j][j : j + 1, :], full)
            inv = 1.0 / pivot
            inverses.append(inv)
            scale = jnp.where(sub == j, pivot, scale)
            m = jnp.where(sub > j, cols[j] * inv, 0.0)
            for k in range(j + 1, SUB):
                uppers[j, k] = jnp.broadcast_to(cols[k][j : j + 1, :], full)
                cols[k] = cols[k] - m * uppers[j, k]
            row = jnp.broadcast_to(current[j : j + 1, :], full)
            row = jnp.where(lane == base + j, 1.0, row)
            finals.append(jnp.where((lane > base + j) & (lane < base + SUB), 0.0, row))
            current = jnp.where((lane == base + j) & (sub >= j), jnp.where(sub == j, 1.0, 0.0), current) - m * row
        inside = (lane >= base) & (lane < base + SUB)
        for i in range(b + 1, count):
            held = [jnp.broadcast_to(rows[i][:, base + j : base + j + 1], full) for j in range(SUB)]
            fresh = jnp.where(inside, 0.0, rows[i])
            for j in range(SUB):
                c = held[j] * inverses[j]
                for k in range(j + 1, SUB):
                    held[k] = held[k] - c * uppers[j, k]
                fresh = fresh - c * finals[j]
            rows[i] = fresh
        rows[b] = jnp.where(lane <= base + sub, current * lax.rsqrt(scale), 0.0)
    return jnp.concatenate(rows, axis=0)


def turned(x):
    return x.astype(jnp.float32).T.astype(x.dtype)


def factor_kernel(bounds_ref, rows_ref, out_ref, right_ref):
    size = out_ref.shape[0]
    count = size // BLOCK
    wide = 2 * BLOCK
    for i in range(size // wide):
        left = turned(rows_ref[:, i * wide : (i + 1) * wide])
        out_ref[i * wide : (i + 1) * wide, i * wide :] = jnp.dot(
            left, rows_ref[:, i * wide :], preferred_element_type=jnp.float32
        )
    across = lax.broadcasted_iota(jnp.int32, (BLOCK, BLOCK), 1)
    eye = lax.broadcasted_iota(jnp.int32, (BLOCK, BLOCK), 0) == across
    kept = bounds_ref[1]
    diagonal = jnp.zeros((BLOCK, BLOCK), jnp.float32)
    for i in range(count):
        here = slice(i * BLOCK, (i + 1) * BLOCK)
        diagonal = diagonal + jnp.where(eye, out_ref[here, here], 0.0)
    trace = jnp.sum(jnp.sum(diagonal, axis=0, keepdims=True), axis=1, keepdims=True)
    ridge = ridge_ratio * trace / jnp.full((1, 1), kept, jnp.int32).astype(jnp.float32)
    for i in range(count):
        here = slice(i * BLOCK, (i + 1) * BLOCK)
        added = jnp.where(across + i * BLOCK < kept, jnp.broadcast_to(ridge, eye.shape), 1.0)
        out_ref[here, here] = out_ref[here, here] + jnp.where(eye, added, 0.0)

    def panel(k, carry):
        here = pl.ds(pl.multiple_of(k * BLOCK, BLOCK), BLOCK)
        inverse = diagonal_inverse(out_ref[here, here])
        inv_high, inv_low = halves(inverse)
        row_high, row_low = halves(out_ref[here, :])
        out_ref[here, :] = jnp.dot(
            jnp.concatenate([inv_high, inv_high, inv_low], axis=1),
            jnp.concatenate([row_high, row_low, row_high], axis=0),
            preferred_element_type=jnp.float32,
        )
        out_ref[here, here] = inverse
        high, low = halves(out_ref[here, :])
        right_ref[0:BLOCK, :] = high
        right_ref[BLOCK : 2 * BLOCK, :] = low
        right_ref[2 * BLOCK : 3 * BLOCK, :] = high

        def trailing(first, height):
            there = pl.ds(pl.multiple_of(first * BLOCK, BLOCK), height)
            left_high, left_low = halves(out_ref[here, there].T)
            out_ref[there, here] = jnp.zeros((height, BLOCK), jnp.float32)
            out_ref[there, :] = out_ref[there, :] - jnp.dot(
                jnp.concatenate([left_high, left_high, left_low], axis=1),
                right_ref[...],
                preferred_element_type=jnp.float32,
            )

        odd = (count - 1 - k) % 2

        @pl.when(odd == 1)
        def _():
            trailing(k + 1, BLOCK)

        def pair(i, inner):
            trailing(k + 1 + odd + 2 * i, wide)
            return inner

        lax.fori_loop(0, (count - 1 - k) // 2, pair, 0)
        column = lax.broadcasted_iota(jnp.int32, (BLOCK, size), 1)
        out_ref[here, :] = jnp.where(column < (k + 1) * BLOCK, out_ref[here, :], 0.0)
        return carry

    lax.fori_loop(0, count, panel, 0)


def factor_inverse(bounds, rows):
    size = rows.shape[1]
    return pl.pallas_call(
        factor_kernel,
        out_shape=jax.ShapeDtypeStruct((size, size), jnp.float32),
        in_specs=[pl.BlockSpec(memory_space=pltpu.SMEM), pl.BlockSpec(memory_space=pltpu.VMEM)],
        out_specs=pl.BlockSpec(memory_space=pltpu.VMEM),
        scratch_shapes=[pltpu.VMEM((3 * BLOCK, size), jnp.bfloat16)],
    )(bounds, rows)


CHUNK = 256


def theta_kernel(gate_ref, bounds_ref, a_ref, b_ref, start_ref, theta_ref, own_ref, image_ref):
    width = start_ref.shape[1]
    height = a_ref.shape[0]
    kept_right, kept_mid, first = bounds_ref[0], bounds_ref[1], bounds_ref[2]
    lane = lax.broadcasted_iota(jnp.int32, (height, CHUNK), 1)

    def mix(c, carry):
        offset = c * CHUNK
        inside = lane + offset < kept_right
        mixed = []
        for i in range(2):
            for j in range(2):
                columns = pl.ds(pl.multiple_of(j * width + offset, CHUNK), CHUNK)
                product = jnp.dot(
                    a_ref[:, i * width : (i + 1) * width],
                    b_ref[:, columns],
                    preferred_element_type=jnp.float32,
                )
                mixed.append(jnp.where(inside, product, 0.0))
        for o in range(2):
            for q in range(2):
                row = 4 * (2 * o + q)
                value = (
                    gate_ref[row] * mixed[0]
                    + gate_ref[row + 1] * mixed[1]
                    + gate_ref[row + 2] * mixed[2]
                    + gate_ref[row + 3] * mixed[3]
                )
                columns = pl.ds(pl.multiple_of(q * width + offset, CHUNK), CHUNK)
                theta_ref[o, :, columns] = value.astype(jnp.bfloat16)
        return carry

    lax.fori_loop(0, width // CHUNK, mix, 0)

    def image(c, carry):
        columns = pl.ds(pl.multiple_of(c * CHUNK, CHUNK), CHUNK)
        total = jnp.dot(
            theta_ref[first, :, :width], start_ref[0, :, columns], preferred_element_type=jnp.float32
        ) + jnp.dot(
            theta_ref[first, :, width:], start_ref[1, :, columns], preferred_element_type=jnp.float32
        )
        image_ref[:, columns] = jnp.where(lane + c * CHUNK < kept_mid, total, 0.0).astype(jnp.bfloat16)
        return carry

    lax.fori_loop(0, width // CHUNK, image, 0)

    def term(c, carry):
        columns = pl.ds(pl.multiple_of(c * CHUNK, CHUNK), CHUNK)
        own_ref[columns, :] = jnp.dot(
            turned(theta_ref[first, :, columns]), image_ref[...], preferred_element_type=jnp.float32
        ).astype(jnp.bfloat16)
        return carry

    lax.fori_loop(0, 2 * width // CHUNK, term, 0)


def theta_terms(gate, bounds, a_used, b_full, starts):
    height, wide = a_used.shape
    width = starts.shape[2]
    return pl.pallas_call(
        theta_kernel,
        out_shape=(
            jax.ShapeDtypeStruct((2, height, wide), jnp.bfloat16),
            jax.ShapeDtypeStruct((wide, width), jnp.bfloat16),
        ),
        in_specs=[pl.BlockSpec(memory_space=pltpu.SMEM)] * 2 + [pl.BlockSpec(memory_space=pltpu.VMEM)] * 3,
        out_specs=(pl.BlockSpec(memory_space=pltpu.VMEM),) * 2,
        scratch_shapes=[pltpu.VMEM((height, width), jnp.bfloat16)],
    )(gate, bounds, a_used, b_full, starts)


MESH = pl.DeviceIdType.MESH


class Links:
    def __init__(self, send_sem, recv_sem):
        self.chain, self.me = lax.axis_index("chain"), lax.axis_index("bond")
        self.core = self.chain % 2
        self.near = self.me + 1 - 2 * (self.me % 2)
        self.far = (self.me + 2) % 4
        self.across = 3 - self.me
        self.x, self.y, self.d = (self.chain, self.near), (self.chain, self.far), (self.chain, self.across)
        self.mate = (self.chain + 1 - 2 * self.core, self.me)
        self.send_sem, self.recv_sem, self.copies = send_sem, recv_sem, []

    def greet(self, others):
        barrier = pltpu.get_barrier_semaphore()
        for other in others:
            pl.semaphore_signal(barrier, inc=1, device_id=other, device_id_type=MESH)
        pl.semaphore_wait(barrier, len(others))

    def send(self, source, target, device):
        slot = len(self.copies)
        copy = pltpu.make_async_remote_copy(
            src_ref=source,
            dst_ref=target,
            send_sem=self.send_sem.at[slot],
            recv_sem=self.recv_sem.at[slot],
            device_id=device,
            device_id_type=MESH,
        )
        copy.start()
        self.copies.append(copy)
        return copy

    def spread(self, first_own, second_own, first, second):
        s0 = self.send(second_own, second(self.me), self.x)
        f0 = self.send(first_own, first(self.me), self.y)
        f1 = self.send(first_own, first(self.me), self.x)
        s1 = self.send(second_own, second(self.me), self.y)
        f0.wait_recv()
        f2 = self.send(first(self.far), first(self.far), self.x)
        late = [self.send(first(self.far), first(self.far), self.mate)]
        s0.wait_recv()
        s2 = self.send(second(self.near), second(self.near), self.y)
        late.append(self.send(second(self.near), second(self.near), self.mate))
        f1.wait_recv()
        late.append(self.send(first(self.near), first(self.near), self.mate))
        s1.wait_recv()
        late.append(self.send(second(self.far), second(self.far), self.mate))
        f2.wait_recv()
        late.append(self.send(first(self.across), first(self.across), self.mate))
        s2.wait_recv()
        late.append(self.send(second(self.across), second(self.across), self.mate))
        for copy in late:
            copy.wait_recv()

    def drain(self):
        for copy in self.copies:
            copy.wait_send()


def gather_kernel(b_ref, s_ref, b_out, s_out, send_sem, recv_sem, local_sem):
    links = Links(send_sem, recv_sem)
    links.greet((links.x, links.y, links.mate))
    core, me = links.core, links.me
    kept_b = pltpu.make_async_copy(b_ref, b_out.at[me], local_sem.at[0])
    kept_s = pltpu.make_async_copy(s_ref, s_out.at[core, me], local_sem.at[1])
    own = links.send(s_ref, s_out.at[core, me], links.mate)
    kept_b.start()
    kept_s.start()
    links.spread(
        b_ref.at[core], s_ref, lambda i: b_out.at[i, core], lambda i: s_out.at[core, i]
    )
    own.wait_recv()
    links.drain()
    kept_b.wait()
    kept_s.wait()


def gather_pair(b_rows, own_start):
    rows, wide = b_rows.shape
    width = own_start.shape[1]
    n = lax.axis_size("bond")
    b_full, starts = pl.pallas_call(
        gather_kernel,
        out_shape=(
            jax.ShapeDtypeStruct((n, 2, rows // 2, wide), b_rows.dtype),
            jax.ShapeDtypeStruct((2, n, rows, width), own_start.dtype),
        ),
        in_specs=[pl.BlockSpec(memory_space=pltpu.VMEM)] * 2,
        out_specs=(pl.BlockSpec(memory_space=pl.ANY),) * 2,
        scratch_shapes=[
            pltpu.SemaphoreType.DMA((13,)),
            pltpu.SemaphoreType.DMA((13,)),
            pltpu.SemaphoreType.DMA((2,)),
        ],
        compiler_params=pltpu.CompilerParams(collective_id=0, has_side_effects=True),
    )(b_rows.reshape(2, rows // 2, wide), own_start)
    return b_full.reshape(n * rows, wide), starts.reshape(2, n * rows, width)


def reduce_kernel(own_ref, out_ref, inc, acc, one, two, send_sem, recv_sem):
    links = Links(send_sem, recv_sem)
    links.greet((links.x, links.y, links.mate))
    core, me, near, far, across = links.core, links.me, links.near, links.far, links.across
    half = own_ref.shape[2] // 2
    low, high = pl.ds(0, half), pl.ds(half, half)
    order = (across, near, far, me)
    swaps = [links.send(own_ref.at[1 - core, i], inc.at[i], links.mate) for i in order]

    def merge(position):
        i = order[position]
        swaps[position].wait_recv()
        acc[i] = (own_ref[core, i].astype(jnp.float32) + inc[i].astype(jnp.float32)).astype(jnp.bfloat16)

    merge(0)
    x1 = links.send(acc.at[across, low], one.at[0, 1], links.x)
    y1 = links.send(acc.at[across, high], one.at[1, 1], links.y)
    merge(1)
    x0 = links.send(acc.at[near, low], one.at[0, 0], links.x)
    merge(2)
    y0 = links.send(acc.at[far, high], one.at[1, 0], links.y)
    merge(3)
    x1.wait_recv()
    two[2] = (acc[far, low].astype(jnp.float32) + one[0, 1].astype(jnp.float32)).astype(jnp.bfloat16)
    y2 = links.send(two.at[2], two.at[0], links.y)
    y1.wait_recv()
    two[3] = (acc[near, high].astype(jnp.float32) + one[1, 1].astype(jnp.float32)).astype(jnp.bfloat16)
    x2 = links.send(two.at[3], two.at[1], links.x)
    x0.wait_recv()
    y2.wait_recv()
    out_ref[core, me, low] = (
        acc[me, low].astype(jnp.float32) + one[0, 0].astype(jnp.float32) + two[0].astype(jnp.float32)
    ).astype(jnp.bfloat16)
    y0.wait_recv()
    x2.wait_recv()
    out_ref[core, me, high] = (
        acc[me, high].astype(jnp.float32) + one[1, 0].astype(jnp.float32) + two[1].astype(jnp.float32)
    ).astype(jnp.bfloat16)
    own = links.send(out_ref.at[core, me], out_ref.at[core, me], links.mate)
    links.spread(
        out_ref.at[core, me, low],
        out_ref.at[core, me, high],
        lambda i: out_ref.at[core, i, low],
        lambda i: out_ref.at[core, i, high],
    )
    own.wait_recv()
    links.drain()


def reduce_pair(own):
    total, width = own.shape
    n = lax.axis_size("bond")
    rows = total // (2 * n)
    whole = pl.pallas_call(
        reduce_kernel,
        out_shape=jax.ShapeDtypeStruct((2, n, rows, width), own.dtype),
        in_specs=[pl.BlockSpec(memory_space=pltpu.VMEM)],
        out_specs=pl.BlockSpec(memory_space=pltpu.VMEM),
        scratch_shapes=[
            pltpu.VMEM((n, rows, width), own.dtype),
            pltpu.VMEM((n, rows, width), own.dtype),
            pltpu.VMEM((2, 2, rows // 2, width), own.dtype),
            pltpu.VMEM((4, rows // 2, width), own.dtype),
            pltpu.SemaphoreType.DMA((23,)),
            pltpu.SemaphoreType.DMA((23,)),
        ],
        compiler_params=pltpu.CompilerParams(collective_id=1, has_side_effects=True),
    )(own.reshape(2, n, rows, width))
    return whole.reshape(total, width)


def total_kernel(value_ref, out_ref, held, send_sem, recv_sem):
    links = Links(send_sem, recv_sem)
    others = (links.x, links.y, links.d)
    links.greet(others)
    copies = [links.send(value_ref, held.at[i], other) for i, other in enumerate(others)]
    for copy in copies:
        copy.wait_recv()
    out_ref[...] = (value_ref[...] + held[2]) + (held[0] + held[1])
    links.drain()


def total_of(value):
    shape = (8, 128)
    return pl.pallas_call(
        total_kernel,
        out_shape=jax.ShapeDtypeStruct(shape, jnp.float32),
        in_specs=[pl.BlockSpec(memory_space=pltpu.VMEM)],
        out_specs=pl.BlockSpec(memory_space=pltpu.VMEM),
        scratch_shapes=[
            pltpu.VMEM((3,) + shape, jnp.float32),
            pltpu.SemaphoreType.DMA((3,)),
            pltpu.SemaphoreType.DMA((3,)),
        ],
        compiler_params=pltpu.CompilerParams(collective_id=2, has_side_effects=True),
    )(jnp.full(shape, value, jnp.float32))[0, 0]


def local(sites, start, gates, bonds):
    bond_index = lax.axis_index("bond")
    chain_index = lax.axis_index("chain")
    rank_width = start.shape[2]
    local_rows = sites.shape[1]
    own_site = sites[0]
    own_start = start[0]
    is_left = chain_index % 2 == 0
    left_site = jnp.where(is_left, chain_index, chain_index - 1)
    bond_left = bonds[left_site]
    bond_mid = bonds[left_site + 1]
    bond_right = bonds[left_site + 2]
    columns = jnp.arange(rank_width)
    row_global = bond_index * local_rows + jnp.arange(local_rows)
    mid_keep = columns < bond_mid
    other_rows = partner(own_site, "chain", 0)
    a_rows = jnp.where(is_left, own_site, other_rows)
    b_rows = jnp.where(is_left, other_rows, own_site)
    square = lax.axis_size("bond") == 4
    if square:
        b_full, starts = gather_pair(b_rows, own_start)
    else:
        b_full = lax.all_gather(b_rows, "bond", axis=0, tiled=True)
        whole_start = lax.all_gather(own_start, "bond", axis=0, tiled=True)
        other_start = partner(whole_start, "chain", 0)
        starts = jnp.stack(
            [jnp.where(is_left, whole_start, other_start), jnp.where(is_left, other_start, whole_start)]
        )
    left_keep = (row_global < bond_left)[:, None] & jnp.tile(mid_keep, 2)[None, :]
    left_used = jnp.where(left_keep, a_rows, jnp.zeros((), jnp.bfloat16))
    bounds = jnp.stack([bond_right, bond_mid, jnp.where(is_left, 0, 1)]).astype(jnp.int32)
    thetas, own = theta_terms(gates[left_site], bounds, left_used, b_full, starts)
    if square:
        projected_all = reduce_pair(own)
    else:
        kept_half = jnp.where(is_left, 0, 1)
        half_rows = own.shape[0] // 2
        kept = lax.dynamic_slice_in_dim(own, kept_half * half_rows, half_rows, 0)
        given = lax.dynamic_slice_in_dim(own, (1 - kept_half) * half_rows, half_rows, 0)
        both = (kept.astype(jnp.float32) + partner(given, "chain", 0).astype(jnp.float32)).astype(jnp.bfloat16)
        summed = lax.psum_scatter(both, "bond", scatter_dimension=0, tiled=True)
        own_half = lax.all_gather(summed, "bond", axis=0, tiled=True)
        other_half = partner(own_half, "chain", 0)
        projected_all = jnp.concatenate(
            [jnp.where(is_left, own_half, other_half), jnp.where(is_left, other_half, own_half)], axis=0
        )
    inverse = factor_inverse(bounds, projected_all)

    def left_rows():
        reduced = jnp.dot(
            thetas.reshape(2 * local_rows, -1), projected_all, preferred_element_type=jnp.float32
        )
        upper = lax.dot_general(
            reduced,
            inverse,
            (((1,), (1,)), ((), ())),
            precision=lax.Precision.HIGH,
            preferred_element_type=jnp.float32,
        )
        joined = jnp.concatenate([upper[:local_rows], upper[local_rows:]], axis=1)
        return joined, jnp.sum(joined * joined)

    def right_rows():
        block = lax.dynamic_slice_in_dim(inverse, bond_index * local_rows, local_rows, 0)
        basis_rows = lax.dot_general(
            block,
            projected_all.astype(jnp.float32),
            (((1,), (1,)), ((), ())),
            precision=lax.Precision.HIGH,
            preferred_element_type=jnp.float32,
        )
        return basis_rows, jnp.float32(0.0)

    rows, squares = lax.cond(is_left, left_rows, right_rows)
    sum_squares = total_of(squares) if square else lax.psum(squares, "bond")
    mean_square = (
        sum_squares / (2.0 * bond_left.astype(jnp.float32) * bond_mid.astype(jnp.float32)) + 1e-06
    )
    factor = jnp.where(
        is_left, lax.rsqrt(mean_square), jnp.sqrt(2.0 * bond_right.astype(jnp.float32))
    )
    return (rows * factor)[None]


def solution(mesh):
    placed = (P("chain", "bond", None), P("chain", "bond", None), P(), P())
    return jax.shard_map(
        local, mesh=mesh, in_specs=placed, out_specs=P("chain", "bond", None), check_vma=False
    )
```

```python
import jax
import jax.numpy as jnp
from jax import lax
from jax.experimental import pallas as pl
from jax.experimental.pallas import tpu as pltpu
from jax.sharding import PartitionSpec as P

ridge_ratio = 0.05
BLOCK = 128
SUB = 8


def partner(value, axis, apart):
    return lax.ppermute(value, axis, [(i, i ^ 1 << apart) for i in range(lax.axis_size(axis))])


def halves(x):
    high = x.astype(jnp.bfloat16)
    return high, (x - high.astype(jnp.float32)).astype(jnp.bfloat16)


def diagonal_inverse(tile):
    lane = lax.broadcasted_iota(jnp.int32, (SUB, BLOCK), 1)
    sub = lax.broadcasted_iota(jnp.int32, (SUB, BLOCK), 0)
    count = BLOCK // SUB
    rows = [tile[i * SUB : (i + 1) * SUB, :] for i in range(count)]
    full = (SUB, BLOCK)
    for b in range(count):
        base = b * SUB
        cols = [jnp.broadcast_to(rows[b][:, base + j : base + j + 1], full) for j in range(SUB)]
        current = rows[b]
        scale = jnp.zeros(full, jnp.float32)
        inverses, uppers, finals = [], {}, []
        for j in range(SUB):
            pivot = jnp.broadcast_to(cols[j][j : j + 1, :], full)
            inv = 1.0 / pivot
            inverses.append(inv)
            scale = jnp.where(sub == j, pivot, scale)
            m = jnp.where(sub > j, cols[j] * inv, 0.0)
            for k in range(j + 1, SUB):
                uppers[j, k] = jnp.broadcast_to(cols[k][j : j + 1, :], full)
                cols[k] = cols[k] - m * uppers[j, k]
            row = jnp.broadcast_to(current[j : j + 1, :], full)
            row = jnp.where(lane == base + j, 1.0, row)
            finals.append(jnp.where((lane > base + j) & (lane < base + SUB), 0.0, row))
            current = jnp.where((lane == base + j) & (sub >= j), jnp.where(sub == j, 1.0, 0.0), current) - m * row
        inside = (lane >= base) & (lane < base + SUB)
        for i in range(b + 1, count):
            held = [jnp.broadcast_to(rows[i][:, base + j : base + j + 1], full) for j in range(SUB)]
            fresh = jnp.where(inside, 0.0, rows[i])
            for j in range(SUB):
                c = held[j] * inverses[j]
                for k in range(j + 1, SUB):
                    held[k] = held[k] - c * uppers[j, k]
                fresh = fresh - c * finals[j]
            rows[i] = fresh
        rows[b] = jnp.where(lane <= base + sub, current * lax.rsqrt(scale), 0.0)
    return jnp.concatenate(rows, axis=0)


def turned(x):
    return x.astype(jnp.float32).T.astype(x.dtype)


def factor_kernel(bounds_ref, rows_ref, out_ref, right_ref):
    size = out_ref.shape[0]
    count = size // BLOCK
    wide = 2 * BLOCK
    for i in range(size // wide):
        left = turned(rows_ref[:, i * wide : (i + 1) * wide])
        out_ref[i * wide : (i + 1) * wide, i * wide :] = jnp.dot(
            left, rows_ref[:, i * wide :], preferred_element_type=jnp.float32
        )
    across = lax.broadcasted_iota(jnp.int32, (BLOCK, BLOCK), 1)
    eye = lax.broadcasted_iota(jnp.int32, (BLOCK, BLOCK), 0) == across
    kept = bounds_ref[1]
    diagonal = jnp.zeros((BLOCK, BLOCK), jnp.float32)
    for i in range(count):
        here = slice(i * BLOCK, (i + 1) * BLOCK)
        diagonal = diagonal + jnp.where(eye, out_ref[here, here], 0.0)
    trace = jnp.sum(jnp.sum(diagonal, axis=0, keepdims=True), axis=1, keepdims=True)
    ridge = ridge_ratio * trace / jnp.full((1, 1), kept, jnp.int32).astype(jnp.float32)
    for i in range(count):
        here = slice(i * BLOCK, (i + 1) * BLOCK)
        added = jnp.where(across + i * BLOCK < kept, jnp.broadcast_to(ridge, eye.shape), 1.0)
        out_ref[here, here] = out_ref[here, here] + jnp.where(eye, added, 0.0)

    def panel(k, carry):
        here = pl.ds(pl.multiple_of(k * BLOCK, BLOCK), BLOCK)
        inverse = diagonal_inverse(out_ref[here, here])
        inv_high, inv_low = halves(inverse)
        row_high, row_low = halves(out_ref[here, :])
        out_ref[here, :] = jnp.dot(
            jnp.concatenate([inv_high, inv_high, inv_low], axis=1),
            jnp.concatenate([row_high, row_low, row_high], axis=0),
            preferred_element_type=jnp.float32,
        )
        out_ref[here, here] = inverse
        high, low = halves(out_ref[here, :])
        right_ref[0:BLOCK, :] = high
        right_ref[BLOCK : 2 * BLOCK, :] = low
        right_ref[2 * BLOCK : 3 * BLOCK, :] = high

        def trailing(first, height):
            there = pl.ds(pl.multiple_of(first * BLOCK, BLOCK), height)
            left_high, left_low = halves(out_ref[here, there].T)
            out_ref[there, here] = jnp.zeros((height, BLOCK), jnp.float32)
            out_ref[there, :] = out_ref[there, :] - jnp.dot(
                jnp.concatenate([left_high, left_high, left_low], axis=1),
                right_ref[...],
                preferred_element_type=jnp.float32,
            )

        odd = (count - 1 - k) % 2

        @pl.when(odd == 1)
        def _():
            trailing(k + 1, BLOCK)

        def pair(i, inner):
            trailing(k + 1 + odd + 2 * i, wide)
            return inner

        lax.fori_loop(0, (count - 1 - k) // 2, pair, 0)
        column = lax.broadcasted_iota(jnp.int32, (BLOCK, size), 1)
        out_ref[here, :] = jnp.where(column < (k + 1) * BLOCK, out_ref[here, :], 0.0)
        return carry

    lax.fori_loop(0, count, panel, 0)


def factor_inverse(bounds, rows):
    size = rows.shape[1]
    return pl.pallas_call(
        factor_kernel,
        out_shape=jax.ShapeDtypeStruct((size, size), jnp.float32),
        in_specs=[pl.BlockSpec(memory_space=pltpu.SMEM), pl.BlockSpec(memory_space=pltpu.VMEM)],
        out_specs=pl.BlockSpec(memory_space=pltpu.VMEM),
        scratch_shapes=[pltpu.VMEM((3 * BLOCK, size), jnp.bfloat16)],
    )(bounds, rows)


CHUNK = 256


def theta_kernel(gate_ref, bounds_ref, a_ref, b_ref, start_ref, theta_ref, own_ref, image_ref):
    width = start_ref.shape[1]
    height = a_ref.shape[0]
    kept_right, kept_mid, first = bounds_ref[0], bounds_ref[1], bounds_ref[2]
    lane = lax.broadcasted_iota(jnp.int32, (height, CHUNK), 1)

    def mix(c, carry):
        offset = c * CHUNK
        inside = lane + offset < kept_right
        mixed = []
        for i in range(2):
            for j in range(2):
                columns = pl.ds(pl.multiple_of(j * width + offset, CHUNK), CHUNK)
                product = jnp.dot(
                    a_ref[:, i * width : (i + 1) * width],
                    b_ref[:, columns],
                    preferred_element_type=jnp.float32,
                )
                mixed.append(jnp.where(inside, product, 0.0))
        for o in range(2):
            for q in range(2):
                row = 4 * (2 * o + q)
                value = (
                    gate_ref[row] * mixed[0]
                    + gate_ref[row + 1] * mixed[1]
                    + gate_ref[row + 2] * mixed[2]
                    + gate_ref[row + 3] * mixed[3]
                )
                columns = pl.ds(pl.multiple_of(q * width + offset, CHUNK), CHUNK)
                theta_ref[o, :, columns] = value.astype(jnp.bfloat16)
        return carry

    lax.fori_loop(0, width // CHUNK, mix, 0)

    def image(c, carry):
        columns = pl.ds(pl.multiple_of(c * CHUNK, CHUNK), CHUNK)
        total = jnp.dot(
            theta_ref[first, :, :width], start_ref[0, :, columns], preferred_element_type=jnp.float32
        ) + jnp.dot(
            theta_ref[first, :, width:], start_ref[1, :, columns], preferred_element_type=jnp.float32
        )
        image_ref[:, columns] = jnp.where(lane + c * CHUNK < kept_mid, total, 0.0).astype(jnp.bfloat16)
        return carry

    lax.fori_loop(0, width // CHUNK, image, 0)

    def term(c, carry):
        columns = pl.ds(pl.multiple_of(c * CHUNK, CHUNK), CHUNK)
        own_ref[columns, :] = jnp.dot(
            turned(theta_ref[first, :, columns]), image_ref[...], preferred_element_type=jnp.float32
        ).astype(jnp.bfloat16)
        return carry

    lax.fori_loop(0, 2 * width // CHUNK, term, 0)


def theta_terms(gate, bounds, a_used, b_full, starts):
    height, wide = a_used.shape
    width = starts.shape[2]
    return pl.pallas_call(
        theta_kernel,
        out_shape=(
            jax.ShapeDtypeStruct((2, height, wide), jnp.bfloat16),
            jax.ShapeDtypeStruct((wide, width), jnp.bfloat16),
        ),
        in_specs=[pl.BlockSpec(memory_space=pltpu.SMEM)] * 2 + [pl.BlockSpec(memory_space=pltpu.VMEM)] * 3,
        out_specs=(pl.BlockSpec(memory_space=pltpu.VMEM),) * 2,
        scratch_shapes=[pltpu.VMEM((height, width), jnp.bfloat16)],
    )(gate, bounds, a_used, b_full, starts)


MESH = pl.DeviceIdType.MESH


class Links:
    def __init__(self, send_sem, recv_sem):
        self.chain, self.me = lax.axis_index("chain"), lax.axis_index("bond")
        self.core = self.chain % 2
        self.near = self.me + 1 - 2 * (self.me % 2)
        self.far = (self.me + 2) % 4
        self.across = 3 - self.me
        self.x, self.y, self.d = (self.chain, self.near), (self.chain, self.far), (self.chain, self.across)
        self.mate = (self.chain + 1 - 2 * self.core, self.me)
        self.send_sem, self.recv_sem, self.copies = send_sem, recv_sem, []

    def greet(self, others):
        barrier = pltpu.get_barrier_semaphore()
        for other in others:
            pl.semaphore_signal(barrier, inc=1, device_id=other, device_id_type=MESH)
        pl.semaphore_wait(barrier, len(others))

    def send(self, source, target, device):
        slot = len(self.copies)
        copy = pltpu.make_async_remote_copy(
            src_ref=source,
            dst_ref=target,
            send_sem=self.send_sem.at[slot],
            recv_sem=self.recv_sem.at[slot],
            device_id=device,
            device_id_type=MESH,
        )
        copy.start()
        self.copies.append(copy)
        return copy

    def spread(self, first_own, second_own, first, second):
        s0 = self.send(second_own, second(self.me), self.x)
        f0 = self.send(first_own, first(self.me), self.y)
        f1 = self.send(first_own, first(self.me), self.x)
        s1 = self.send(second_own, second(self.me), self.y)
        f0.wait_recv()
        f2 = self.send(first(self.far), first(self.far), self.x)
        late = [self.send(first(self.far), first(self.far), self.mate)]
        s0.wait_recv()
        s2 = self.send(second(self.near), second(self.near), self.y)
        late.append(self.send(second(self.near), second(self.near), self.mate))
        f1.wait_recv()
        late.append(self.send(first(self.near), first(self.near), self.mate))
        s1.wait_recv()
        late.append(self.send(second(self.far), second(self.far), self.mate))
        f2.wait_recv()
        late.append(self.send(first(self.across), first(self.across), self.mate))
        s2.wait_recv()
        late.append(self.send(second(self.across), second(self.across), self.mate))
        for copy in late:
            copy.wait_recv()

    def drain(self):
        for copy in self.copies:
            copy.wait_send()


def gather_kernel(b_ref, s_ref, b_out, s_out, send_sem, recv_sem, local_sem):
    links = Links(send_sem, recv_sem)
    links.greet((links.x, links.y, links.mate))
    core, me = links.core, links.me
    kept_b = pltpu.make_async_copy(b_ref, b_out.at[me], local_sem.at[0])
    kept_s = pltpu.make_async_copy(s_ref, s_out.at[core, me], local_sem.at[1])
    own = links.send(s_ref, s_out.at[core, me], links.mate)
    kept_b.start()
    kept_s.start()
    links.spread(
        b_ref.at[core], s_ref, lambda i: b_out.at[i, core], lambda i: s_out.at[core, i]
    )
    own.wait_recv()
    links.drain()
    kept_b.wait()
    kept_s.wait()


def gather_pair(b_rows, own_start):
    rows, wide = b_rows.shape
    width = own_start.shape[1]
    n = lax.axis_size("bond")
    b_full, starts = pl.pallas_call(
        gather_kernel,
        out_shape=(
            jax.ShapeDtypeStruct((n, 2, rows // 2, wide), b_rows.dtype),
            jax.ShapeDtypeStruct((2, n, rows, width), own_start.dtype),
        ),
        in_specs=[pl.BlockSpec(memory_space=pltpu.VMEM)] * 2,
        out_specs=(pl.BlockSpec(memory_space=pl.ANY),) * 2,
        scratch_shapes=[
            pltpu.SemaphoreType.DMA((13,)),
            pltpu.SemaphoreType.DMA((13,)),
            pltpu.SemaphoreType.DMA((2,)),
        ],
        compiler_params=pltpu.CompilerParams(collective_id=0, has_side_effects=True),
    )(b_rows.reshape(2, rows // 2, wide), own_start)
    return b_full.reshape(n * rows, wide), starts.reshape(2, n * rows, width)


def reduce_kernel(own_ref, out_ref, inc, acc, one, two, send_sem, recv_sem):
    links = Links(send_sem, recv_sem)
    links.greet((links.x, links.y, links.mate))
    core, me, near, far, across = links.core, links.me, links.near, links.far, links.across
    half = own_ref.shape[2] // 2
    low, high = pl.ds(0, half), pl.ds(half, half)
    order = (across, near, far, me)
    swaps = [links.send(own_ref.at[1 - core, i], inc.at[i], links.mate) for i in order]

    def merge(position):
        i = order[position]
        swaps[position].wait_recv()
        acc[i] = (own_ref[core, i].astype(jnp.float32) + inc[i].astype(jnp.float32)).astype(jnp.bfloat16)

    merge(0)
    x1 = links.send(acc.at[across, low], one.at[0, 1], links.x)
    y1 = links.send(acc.at[across, high], one.at[1, 1], links.y)
    merge(1)
    x0 = links.send(acc.at[near, low], one.at[0, 0], links.x)
    merge(2)
    y0 = links.send(acc.at[far, high], one.at[1, 0], links.y)
    merge(3)
    x1.wait_recv()
    two[2] = (acc[far, low].astype(jnp.float32) + one[0, 1].astype(jnp.float32)).astype(jnp.bfloat16)
    y2 = links.send(two.at[2], two.at[0], links.y)
    y1.wait_recv()
    two[3] = (acc[near, high].astype(jnp.float32) + one[1, 1].astype(jnp.float32)).astype(jnp.bfloat16)
    x2 = links.send(two.at[3], two.at[1], links.x)
    x0.wait_recv()
    y2.wait_recv()
    out_ref[core, me, low] = (
        acc[me, low].astype(jnp.float32) + one[0, 0].astype(jnp.float32) + two[0].astype(jnp.float32)
    ).astype(jnp.bfloat16)
    y0.wait_recv()
    x2.wait_recv()
    out_ref[core, me, high] = (
        acc[me, high].astype(jnp.float32) + one[1, 0].astype(jnp.float32) + two[1].astype(jnp.float32)
    ).astype(jnp.bfloat16)
    own = links.send(out_ref.at[core, me], out_ref.at[core, me], links.mate)
    links.spread(
        out_ref.at[core, me, low],
        out_ref.at[core, me, high],
        lambda i: out_ref.at[core, i, low],
        lambda i: out_ref.at[core, i, high],
    )
    own.wait_recv()
    links.drain()


def reduce_pair(own):
    total, width = own.shape
    n = lax.axis_size("bond")
    rows = total // (2 * n)
    whole = pl.pallas_call(
        reduce_kernel,
        out_shape=jax.ShapeDtypeStruct((2, n, rows, width), own.dtype),
        in_specs=[pl.BlockSpec(memory_space=pltpu.VMEM)],
        out_specs=pl.BlockSpec(memory_space=pltpu.VMEM),
        scratch_shapes=[
            pltpu.VMEM((n, rows, width), own.dtype),
            pltpu.VMEM((n, rows, width), own.dtype),
            pltpu.VMEM((2, 2, rows // 2, width), own.dtype),
            pltpu.VMEM((4, rows // 2, width), own.dtype),
            pltpu.SemaphoreType.DMA((23,)),
            pltpu.SemaphoreType.DMA((23,)),
        ],
        compiler_params=pltpu.CompilerParams(collective_id=1, has_side_effects=True),
    )(own.reshape(2, n, rows, width))
    return whole.reshape(total, width)


def total_kernel(value_ref, out_ref, held, send_sem, recv_sem):
    links = Links(send_sem, recv_sem)
    others = (links.x, links.y, links.d)
    links.greet(others)
    copies = [links.send(value_ref, held.at[i], other) for i, other in enumerate(others)]
    for copy in copies:
        copy.wait_recv()
    out_ref[...] = (value_ref[...] + held[2]) + (held[0] + held[1])
    links.drain()


def total_of(value):
    shape = (8, 128)
    return pl.pallas_call(
        total_kernel,
        out_shape=jax.ShapeDtypeStruct(shape, jnp.float32),
        in_specs=[pl.BlockSpec(memory_space=pltpu.VMEM)],
        out_specs=pl.BlockSpec(memory_space=pltpu.VMEM),
        scratch_shapes=[
            pltpu.VMEM((3,) + shape, jnp.float32),
            pltpu.SemaphoreType.DMA((3,)),
            pltpu.SemaphoreType.DMA((3,)),
        ],
        compiler_params=pltpu.CompilerParams(collective_id=2, has_side_effects=True),
    )(jnp.full(shape, value, jnp.float32))[:1, :1]


def local(sites, start, gates, bonds):
    bond_index = lax.axis_index("bond")
    chain_index = lax.axis_index("chain")
    rank_width = start.shape[2]
    local_rows = sites.shape[1]
    own_site = sites[0]
    own_start = start[0]
    is_left = chain_index % 2 == 0
    left_site = jnp.where(is_left, chain_index, chain_index - 1)
    bond_left = bonds[left_site]
    bond_mid = bonds[left_site + 1]
    bond_right = bonds[left_site + 2]
    columns = jnp.arange(rank_width)
    row_global = bond_index * local_rows + jnp.arange(local_rows)
    mid_keep = columns < bond_mid
    other_rows = partner(own_site, "chain", 0)
    a_rows = jnp.where(is_left, own_site, other_rows)
    b_rows = jnp.where(is_left, other_rows, own_site)
    square = lax.axis_size("bond") == 4
    if square:
        b_full, starts = gather_pair(b_rows, own_start)
    else:
        b_full = lax.all_gather(b_rows, "bond", axis=0, tiled=True)
        whole_start = lax.all_gather(own_start, "bond", axis=0, tiled=True)
        other_start = partner(whole_start, "chain", 0)
        starts = jnp.stack(
            [jnp.where(is_left, whole_start, other_start), jnp.where(is_left, other_start, whole_start)]
        )
    left_keep = (row_global < bond_left)[:, None] & jnp.tile(mid_keep, 2)[None, :]
    left_used = jnp.where(left_keep, a_rows, jnp.zeros((), jnp.bfloat16))
    bounds = jnp.stack([bond_right, bond_mid, jnp.where(is_left, 0, 1)]).astype(jnp.int32)
    thetas, own = theta_terms(gates[left_site], bounds, left_used, b_full, starts)
    if square:
        projected_all = reduce_pair(own)
    else:
        kept_half = jnp.where(is_left, 0, 1)
        half_rows = own.shape[0] // 2
        kept = lax.dynamic_slice_in_dim(own, kept_half * half_rows, half_rows, 0)
        given = lax.dynamic_slice_in_dim(own, (1 - kept_half) * half_rows, half_rows, 0)
        both = (kept.astype(jnp.float32) + partner(given, "chain", 0).astype(jnp.float32)).astype(jnp.bfloat16)
        summed = lax.psum_scatter(both, "bond", scatter_dimension=0, tiled=True)
        own_half = lax.all_gather(summed, "bond", axis=0, tiled=True)
        other_half = partner(own_half, "chain", 0)
        projected_all = jnp.concatenate(
            [jnp.where(is_left, own_half, other_half), jnp.where(is_left, other_half, own_half)], axis=0
        )
    inverse = factor_inverse(bounds, projected_all)

    def left_rows():
        reduced = jnp.dot(
            thetas.reshape(2 * local_rows, -1), projected_all, preferred_element_type=jnp.float32
        )
        upper = lax.dot_general(
            reduced,
            inverse,
            (((1,), (1,)), ((), ())),
            precision=lax.Precision.HIGH,
            preferred_element_type=jnp.float32,
        )
        joined = jnp.concatenate([upper[:local_rows], upper[local_rows:]], axis=1)
        return joined, jnp.sum(joined * joined)

    def right_rows():
        block = lax.dynamic_slice_in_dim(inverse, bond_index * local_rows, local_rows, 0)
        basis_rows = lax.dot_general(
            block,
            projected_all.astype(jnp.float32),
            (((1,), (1,)), ((), ())),
            precision=lax.Precision.HIGH,
            preferred_element_type=jnp.float32,
        )
        return basis_rows, jnp.float32(0.0)

    rows, squares = lax.cond(is_left, left_rows, right_rows)
    sum_squares = total_of(squares) if square else lax.psum(squares, "bond")
    mean_square = (
        sum_squares / (2.0 * bond_left.astype(jnp.float32) * bond_mid.astype(jnp.float32)) + 1e-06
    )
    factor = jnp.where(
        jnp.full(jnp.shape(mean_square), is_left), lax.rsqrt(mean_square), jnp.sqrt(2.0 * bond_right.astype(jnp.float32))
    )
    return (rows * factor)[None]


def solution(mesh):
    placed = (P("chain", "bond", None), P("chain", "bond", None), P(), P())
    return jax.shard_map(
        local, mesh=mesh, in_specs=placed, out_specs=P("chain", "bond", None), check_vma=False
    )
```
